32 devices in a mesh: rep: 4 (over y, x), mp: 8 (over z, core).
Axes of the slice: x: 2, y: 2, z: 4, core: 2. Of those that a mesh axis runs over, the one named last changes fastest.
Arguments:
- acts: bfloat16 [1024, 64, 256], P('rep', 'mp'), may hold values from -40 to 40, as said below
- refresh: int32 [64], P(('mp', 'rep')), may hold values from 0 to 8, as said below
- damping: float32 [64], P(('mp', 'rep')), may hold values from 0.2 to 1
- old_inverse: bfloat16 [64, 256, 256], P(('mp', 'rep')), may hold values from -0.375 to 0.375
- grads: bfloat16 [1024, 64, 256], P('rep', 'mp'), may hold values from -6 to 6
Outputs:
- covariance: float32 [64, 256, 256], P(('mp', 'rep'))
- new_inverse: bfloat16 [64, 256, 256], P(('mp', 'rep'))
- precond: bfloat16 [1024, 64, 256], P('rep', 'mp')
The draws below stay inside these ranges and needn't reach their ends.
Inputs may be any that keep to these rules, and one draw needn't show every extreme that they name: `acts`: entries are bfloat16 values of order one with unequal feature scales. Block g * 8 + 2 * r + q (q = 0 or 1) is the q-th block of group g at replica index r. A block is refreshed only by a group through the same r. For every r, each group refreshes exactly one block through r. Of the two blocks of a group at r, at most one is refreshed by another group, and then the other one by the group itself. In every draw some groups refresh a block of another group.
All inputs are finite; a program needn't handle non-finite values. Where the reference program divides by a largest or mean magnitude, that divisor is 1e-20 or more.
Results may differ from the reference program's by a relative error of at most 0.009.
Values may be sent and summed in bfloat16 or wider, within the bound.
A program may use at most 64 MiB of HBM per device.

```python
import math
import jax
import jax.numpy as jnp
from jax import lax

B = 256
OUT = 1024
ITERS = 5
BLK_DEV = 8
GROUPS = 8
TOKENS = 1024
NBLK = 64


def draw_acts(key, part):

    def one_block(block_index):
        block_key = jax.random.fold_in(jax.random.fold_in(key, 7), block_index)
        key_list = jax.random.split(block_key, 3)
        base_noise = jax.random.normal(key_list[0], (TOKENS, B), jnp.float32)
        scales = jnp.exp(jax.random.uniform(key_list[2], (B,), jnp.float32, jnp.log(0.5), jnp.log(2.0)))
        feature_order = jax.random.permutation(key_list[1], B)
        mixed = base_noise + 0.7 * jnp.take(base_noise, feature_order, axis=1)
        return (mixed * scales[None, :]).astype(jnp.bfloat16)
    blocks = lax.map(one_block, jnp.arange(NBLK, dtype=jnp.int32))
    return jnp.transpose(blocks, (1, 0, 2))


def draw_refresh(key, part):
    replicas = BLK_DEV // 2
    heavy_count = GROUPS * 3 // 8
    key_list = jax.random.split(jax.random.fold_in(key, 23), 2)
    row_keys = jax.random.split(key_list[0], replicas)
    arranged = jax.vmap(lambda row_key: jax.random.permutation(row_key, GROUPS))(row_keys).astype(jnp.int32)
    position = jnp.argsort(arranged, axis=1, stable=True).astype(jnp.int32)
    local_pick = jax.random.randint(key_list[1], (replicas, GROUPS), 0, 2)
    partner = jnp.take_along_axis(arranged, jnp.minimum(position + heavy_count, GROUPS - 1), axis=1)
    own_group = jnp.broadcast_to(jnp.arange(GROUPS, dtype=jnp.int32)[None, :], (replicas, GROUPS))
    is_giver = position < heavy_count
    is_taker = (position >= heavy_count) & (position < 2 * heavy_count)
    other_value = jnp.where(is_giver, partner, GROUPS)
    first_value = jnp.where(local_pick == 0, own_group, other_value)
    second_value = jnp.where(local_pick == 1, own_group, other_value)
    first_value = jnp.where(is_taker, GROUPS, first_value)
    second_value = jnp.where(is_taker, GROUPS, second_value)
    stacked = jnp.stack([first_value, second_value], axis=-1)
    return jnp.transpose(stacked, (1, 0, 2)).reshape(NBLK).astype(jnp.int32)


def levels(rng, shape, cuts, least, top_value):
    gain = 1.0
    for dim, shards_of in cuts:
        heights = jax.random.uniform(jax.random.fold_in(jax.random.fold_in(rng, 6), dim), (shards_of,), jnp.float32, least / len(cuts), top_value / len(cuts))
        gain = gain * jnp.repeat(jnp.exp(heights), shape[dim] // shards_of).reshape((-1,) + (1,) * (len(shape) - 1 - dim))
    return gain


def scatter_about(stream_key, shape, width, most, cuts=(), kind=jnp.bfloat16):
    factor_of = levels(stream_key, shape, cuts, -0.22, 0.18) if cuts else 1.0
    values = jax.random.normal(stream_key, shape, jnp.float32) * width * factor_of
    return jnp.minimum(jnp.maximum(values, -most), most).astype(kind)


def setup_inputs(seed: int = 0) -> dict:
    arg_keys = jax.random.split(jax.random.key(seed), 6)
    return {
        "acts": draw_acts(jax.random.fold_in(arg_keys[5], 71), 0),
        "refresh": draw_refresh(jax.random.fold_in(arg_keys[5], 71), 0),
        "damping": jnp.clip(jnp.exp(math.log(1.0) - 1.609438 * jax.random.uniform(arg_keys[2], (NBLK,), jnp.float32) ** levels(arg_keys[2], (NBLK,), ((0, 32),), -0.2, 0.2)), 0.2, 1.0),
        "old_inverse": scatter_about(arg_keys[3], (NBLK, B, B), B ** -0.5, 0.375, ((0, 32),)),
        "grads": scatter_about(arg_keys[4], (OUT, NBLK, B), 1.0, 6.0, ((0, 4), (1, 8))),
    }


HIGHEST_PRECISION = lax.Precision.HIGHEST


def newton_inverse(gram, damp_value):
    order_size = gram.shape[-1]
    identity = jnp.eye(order_size, dtype=jnp.float32)
    matrix = gram + damp_value * identity
    row_bound = jnp.max(jnp.sum(jnp.abs(matrix), axis=1))
    approx = identity / row_bound
    for iteration in range(ITERS):
        product = jnp.dot(matrix, approx, precision=HIGHEST_PRECISION, preferred_element_type=jnp.float32)
        approx = jnp.dot(approx, 2.0 * identity - product, precision=HIGHEST_PRECISION, preferred_element_type=jnp.float32)
    return approx


def reference(acts, refresh, damping, old_inverse, grads):
    def block_gram(block_index):
        block_acts = lax.dynamic_index_in_dim(acts, block_index, 1, keepdims=False)
        return jnp.dot(block_acts.T, block_acts, preferred_element_type=jnp.float32) / TOKENS

    covariance = lax.map(block_gram, jnp.arange(NBLK, dtype=jnp.int32))

    def invert_one(inputs_pair):
        return newton_inverse(inputs_pair[0], inputs_pair[1]).astype(jnp.bfloat16)

    refreshed = lax.map(invert_one, (covariance, damping))
    due_mask = refresh != GROUPS
    new_inverse = jnp.where(due_mask[:, None, None], refreshed, old_inverse)

    def precondition(block_index):
        grad_block = lax.dynamic_index_in_dim(grads, block_index, 1, keepdims=False)
        inverse = lax.dynamic_index_in_dim(new_inverse, block_index, 0, keepdims=False)
        return jnp.dot(grad_block, inverse, preferred_element_type=jnp.float32).astype(jnp.bfloat16)

    precond = lax.map(precondition, jnp.arange(NBLK, dtype=jnp.int32))
    return covariance, new_inverse, jnp.transpose(precond, (1, 0, 2))
```

```python
import functools

import jax
import jax.numpy as jnp
from jax import lax
from jax.experimental import pallas as pl
from jax.experimental.pallas import tpu as pltpu
from jax.sharding import PartitionSpec as P

ITERS = 5
MESH = pl.DeviceIdType.MESH
F32 = jnp.float32
BF16 = jnp.bfloat16


def split(x):
    high = x.astype(BF16)
    return high, (x - high.astype(F32)).astype(BF16)


def dot3(lhs, rhs):
    lh, ll = lhs
    rh, rl = rhs
    mm = functools.partial(jnp.dot, preferred_element_type=F32)
    return mm(lh, rh) + (mm(lh, rl) + mm(ll, rh))


def partner(me, step, n):
    if n & (n - 1):
        return lax.rem(me + step, n), lax.rem(me + n - step, n)
    other = me
    bit = 1
    while bit < n:
        if step & bit:
            other = other + bit * (1 - 2 * lax.rem(me // bit, 2))
        bit *= 2
    return other, other


def kernel(
    n,
    held,
    groups,
    tokens_all,
    acts_hbm,
    refresh_ref,
    damping_ref,
    old_hbm,
    grads_hbm,
    cov_ref,
    inv_ref,
    pre_ref,
    acts_v,
    grads_v,
    old_v,
    acts_f,
    grads_f,
    pre_f,
    own_f,
    out_buf,
    in_buf,
    gathered,
    load_sem,
    rs_send,
    rs_recv,
    ag_send,
    ag_recv,
):
    me = lax.axis_index("rep")
    blocks = n * held
    order = inv_ref.shape[-1]
    half = order // 2
    rows = acts_v.shape[0] // blocks
    relay = n == 4
    halves = order // 2

    barrier = pltpu.get_barrier_semaphore()
    for step in range(1, n):
        pl.semaphore_signal(
            barrier, inc=1, device_id={"rep": partner(me, step, n)[0]}, device_id_type=MESH
        )

    loads = [
        pltpu.make_async_copy(acts_hbm, acts_v, load_sem.at[0]),
        pltpu.make_async_copy(grads_hbm, grads_v, load_sem.at[1]),
        pltpu.make_async_copy(old_hbm, old_v, load_sem.at[2]),
    ]
    for load in loads:
        load.start()

    row_id = lax.broadcasted_iota(jnp.int32, (half, half), 0)
    col_id = lax.broadcasted_iota(jnp.int32, (half, half), 1)
    upper = col_id >= row_id
    on_diag = col_id == row_id

    def widen(source, target):
        for tile in range(order // 128):
            target[tile] = source[:, tile * 128 : (tile + 1) * 128].astype(F32)

    def take(source, block):
        return jnp.concatenate(
            [
                source[tile, pl.ds(block, rows, stride=blocks), :]
                for tile in range(order // 128)
            ],
            axis=1,
        ).astype(BF16)

    def gram(block):
        part = take(acts_f, block)
        full = lax.dot_general(
            part, part, (((0,), (0,)), ((), ())), preferred_element_type=F32
        )
        low = full[half:, half:]
        last = jnp.sum(jnp.where(on_diag, low, 0.0), axis=0, keepdims=True)
        return full[:half, half:], jnp.where(upper, full[:half, :half], low), last

    loads[0].wait()
    widen(acts_v, acts_f)

    rs = {}
    greeted = False
    steps = list(range(n - 1, 0, -1))
    for slot in range(held):
        for step in steps:
            target = partner(me, step, n)[0]
            cross, packed, last = gram(target * held + slot)
            place = out_buf.at[step - 1, slot]
            place[:half, :] = cross.astype(BF16)
            place[half : 2 * half, :] = packed.astype(BF16)
            place[2 * half :, :] = jnp.broadcast_to(last, (16, half)).astype(BF16)
            if not greeted:
                pl.semaphore_wait(barrier, n - 1)
                greeted = True
            copy = pltpu.make_async_remote_copy(
                src_ref=place,
                dst_ref=in_buf.at[step - 1, slot],
                send_sem=rs_send.at[step - 1, slot],
                recv_sem=rs_recv.at[step - 1, slot],
                device_id={"rep": target},
                device_id_type=MESH,
            )
            copy.start()
            rs[step, slot] = copy
        cross, packed, last = gram(me * held + slot)
        own_f[slot, :half, :] = cross
        own_f[slot, half : 2 * half, :] = packed
        own_f[slot, 2 * half :, :] = jnp.broadcast_to(last, (8, half))

    loads[1].wait()
    widen(grads_v, grads_f)
    loads[2].wait()

    eye = jnp.where(
        lax.broadcasted_iota(jnp.int32, (order, order), 0)
        == lax.broadcasted_iota(jnp.int32, (order, order), 1),
        1.0,
        0.0,
    ).astype(F32)

    ag = {}

    def ship(key, source, target, step, sem):
        copy = pltpu.make_async_remote_copy(
            src_ref=source,
            dst_ref=target,
            send_sem=ag_send.at[sem],
            recv_sem=ag_recv.at[sem],
            device_id={"rep": partner(me, step, n)[0]},
            device_id_type=MESH,
        )
        copy.start()
        ag[key] = copy

    def refresh_block(slot):
        total = own_f[slot]
        total_cross, total_packed, total_last = (
            total[:half],
            total[half : 2 * half],
            total[2 * half : 2 * half + 1],
        )
        for step in steps:
            rs[step, slot].wait_recv()
            came = in_buf[step - 1, slot].astype(F32)
            total_cross = total_cross + came[:half]
            total_packed = total_packed + came[half : 2 * half]
            total_last = total_last + came[2 * half : 2 * half + 1]
        scale = 1.0 / tokens_all
        flipped = total_packed.T
        first = jnp.where(upper, total_packed, flipped)
        second = jnp.where(
            on_diag,
            jnp.broadcast_to(total_last, (half, half)),
            jnp.where(upper, flipped, total_packed),
        )
        covariance = (
            jnp.concatenate(
                [
                    jnp.concatenate([first, total_cross], axis=1),
                    jnp.concatenate([total_cross.T, second], axis=1),
                ],
                axis=0,
            )
            * scale
        )
        cov_ref[slot] = covariance
        matrix = covariance + damping_ref[slot] * eye
        bound = jnp.max(jnp.sum(jnp.abs(matrix), axis=0, keepdims=True), axis=1, keepdims=True)
        inverse_bound = 1.0 / bound
        residual = eye - matrix * inverse_bound
        series = eye + residual
        power = split(residual)
        power = split(dot3(power, power))
        for iteration in range(2, ITERS):
            left = split(series)
            square = dot3(power, power)
            series = series + dot3(left, power)
            power = split(square)
        series = series + dot3(split(series), power)
        approx = (series * inverse_bound).astype(BF16)
        due = jnp.full((order, order), refresh_ref[slot], jnp.int32) != groups
        chosen = jnp.where(due, approx, old_v[slot])
        inv_ref[slot] = chosen
        gathered[0, slot] = chosen
        if relay:
            top, bottom = pl.ds(0, halves), pl.ds(halves, halves)
            for part, (step, piece) in enumerate(((1, top), (2, bottom), (1, bottom), (2, top))):
                ship(
                    (slot, part),
                    gathered.at[0, slot, piece],
                    gathered.at[step, slot, piece],
                    step,
                    slot * 6 + part,
                )
        else:
            for step in steps:
                ship(
                    (slot, step),
                    gathered.at[0, slot],
                    gathered.at[step, slot],
                    step,
                    slot * 6 * n + step,
                )

    def forward(slot):
        top, bottom = pl.ds(0, halves), pl.ds(halves, halves)
        ag[slot, 0].wait_recv()
        ship((slot, 4), gathered.at[1, slot, top], gathered.at[3, slot, top], 2, slot * 6 + 4)
        ag[slot, 1].wait_recv()
        ship((slot, 5), gathered.at[2, slot, bottom], gathered.at[3, slot, bottom], 1, slot * 6 + 5)

    def apply(step, slot):
        block = partner(me, step, n)[1] * held + slot
        result = jnp.dot(
            take(grads_f, block), gathered[step, slot], preferred_element_type=F32
        )
        for tile in range(order // 128):
            pre_f[tile, pl.ds(block, rows, stride=blocks), :] = result[
                :, tile * 128 : (tile + 1) * 128
            ]

    for slot in range(held):
        refresh_block(slot)
        if relay and slot > 0:
            forward(slot - 1)
    if relay:
        forward(held - 1)
    for slot in range(held):
        apply(0, slot)
    for slot in range(held):
        if relay:
            ag[slot, 2].wait_recv()
            apply(1, slot)
            ag[slot, 3].wait_recv()
            apply(2, slot)
            ag[slot, 4].wait_recv()
            ag[slot, 5].wait_recv()
            apply(3, slot)
        else:
            for step in steps:
                ag[slot, step].wait_recv()
                apply(step, slot)
    for tile in range(order // 128):
        pre_ref[:, tile * 128 : (tile + 1) * 128] = pre_f[tile].astype(BF16)
    for copy in rs.values():
        copy.wait_send()
    for copy in ag.values():
        copy.wait_send()


def local(acts, refresh, damping, old_inverse, grads):
    n = lax.axis_size("rep")
    groups = lax.axis_size("mp")
    rows, blocks, order = acts.shape
    grad_rows = grads.shape[0]
    held = refresh.shape[0]
    half = order // 2
    tiles = order // 128
    copies = held * 6 if n == 4 else held * 6 * n
    any_space = pl.BlockSpec(memory_space=pl.ANY)
    smem = pl.BlockSpec(memory_space=pltpu.SMEM)
    vmem = pl.BlockSpec(memory_space=pltpu.VMEM)
    covariance, new_inverse, precond = pl.pallas_call(
        functools.partial(kernel, n, held, groups, rows * n),
        out_shape=(
            jax.ShapeDtypeStruct((held, order, order), F32),
            jax.ShapeDtypeStruct((held, order, order), BF16),
            jax.ShapeDtypeStruct((grad_rows * blocks, order), BF16),
        ),
        in_specs=[any_space, smem, smem, any_space, any_space],
        out_specs=(vmem, vmem, vmem),
        scratch_shapes=[
            pltpu.VMEM((rows * blocks, order), BF16),
            pltpu.VMEM((grad_rows * blocks, order), BF16),
            pltpu.VMEM((held, order, order), BF16),
            pltpu.VMEM((tiles, rows * blocks, 128), F32),
            pltpu.VMEM((tiles, grad_rows * blocks, 128), F32),
            pltpu.VMEM((tiles, grad_rows * blocks, 128), F32),
            pltpu.VMEM((held, order + 8, half), F32),
            pltpu.VMEM((n - 1, held, order + 16, half), BF16),
            pltpu.VMEM((n - 1, held, order + 16, half), BF16),
            pltpu.VMEM((n, held, order, order), BF16),
            pltpu.SemaphoreType.DMA((3,)),
            pltpu.SemaphoreType.DMA((n - 1, held)),
            pltpu.SemaphoreType.DMA((n - 1, held)),
            pltpu.SemaphoreType.DMA((copies,)),
            pltpu.SemaphoreType.DMA((copies,)),
        ],
        compiler_params=pltpu.CompilerParams(
            collective_id=0, has_side_effects=True, vmem_limit_bytes=63 << 20
        ),
    )(
        acts.reshape(rows * blocks, order),
        refresh,
        damping,
        old_inverse,
        grads.reshape(grad_rows * blocks, order),
    )
    return covariance, new_inverse, precond.reshape(grad_rows, blocks, order)


def solution(mesh):
    return jax.shard_map(
        local,
        mesh=mesh,
        in_specs=(
            P("rep", "mp", None),
            P(("mp", "rep")),
            P(("mp", "rep")),
            P(("mp", "rep"), None, None),
            P("rep", "mp", None),
        ),
        out_specs=(
            P(("mp", "rep"), None, None),
            P(("mp", "rep"), None, None),
            P("rep", "mp", None),
        ),
        check_vma=False,
    )
```

```python
import functools
import math

import jax
import jax.numpy as jnp
from jax import lax
from jax.experimental import pallas as pl
from jax.experimental.pallas import tpu as pltpu
from jax.sharding import PartitionSpec as P

ITERS = 5
CHUNKS = 4
MESH = pl.DeviceIdType.MESH
F32 = jnp.float32
BF16 = jnp.bfloat16


def split(x):
    high = x.astype(BF16)
    return high, (x - high.astype(F32)).astype(BF16)


def dot3(lhs, rhs):
    lh, ll = lhs
    rh, rl = rhs
    mm = functools.partial(jnp.dot, preferred_element_type=F32)
    return mm(lh, rh) + (mm(lh, rl) + mm(ll, rh))


def partner(me, step, n):
    if n & (n - 1):
        return lax.rem(me + step, n), lax.rem(me + n - step, n)
    other = me
    bit = 1
    while bit < n:
        if step & bit:
            other = other + bit * (1 - 2 * lax.rem(me // bit, 2))
        bit *= 2
    return other, other


def kernel(
    n,
    held,
    groups,
    tokens_all,
    acts_hbm,
    refresh_ref,
    damping_ref,
    old_hbm,
    grads_hbm,
    cov_ref,
    inv_ref,
    pre_f,
    acts_v,
    grads_v,
    old_v,
    acts_f,
    grads_f,
    own_f,
    out_buf,
    in_buf,
    gathered,
    load_sem,
    rs_send,
    rs_recv,
    ag_send,
    ag_recv,
):
    me = lax.axis_index("rep")
    blocks = n * held
    order = inv_ref.shape[-1]
    half = order // 2
    rows = acts_v.shape[0] // blocks
    relay = n == 4
    halves = order // 2

    barrier = pltpu.get_barrier_semaphore()
    for step in range(1, n):
        pl.semaphore_signal(
            barrier, inc=1, device_id={"rep": partner(me, step, n)[0]}, device_id_type=MESH
        )

    loads = [
        pltpu.make_async_copy(acts_hbm, acts_v, load_sem.at[0]),
        pltpu.make_async_copy(grads_hbm, grads_v, load_sem.at[1]),
        pltpu.make_async_copy(old_hbm, old_v, load_sem.at[2]),
    ]
    for load in loads:
        load.start()

    row_id = lax.broadcasted_iota(jnp.int32, (half, half), 0)
    col_id = lax.broadcasted_iota(jnp.int32, (half, half), 1)
    upper = col_id >= row_id
    on_diag = col_id == row_id

    def widen(source, target):
        for tile in range(order // 128):
            target[tile] = source[:, tile * 128 : (tile + 1) * 128].astype(F32)

    def take(source, block):
        return jnp.concatenate(
            [
                source[tile, pl.ds(block, rows, stride=blocks), :]
                for tile in range(order // 128)
            ],
            axis=1,
        ).astype(BF16)

    def gram(block):
        part = take(acts_f, block)
        full = lax.dot_general(
            part, part, (((0,), (0,)), ((), ())), preferred_element_type=F32
        )
        low = full[half:, half:]
        last = jnp.sum(jnp.where(on_diag, low, 0.0), axis=0, keepdims=True)
        return full[:half, half:], jnp.where(upper, full[:half, :half], low), last

    loads[0].wait()
    widen(acts_v, acts_f)

    rs = {}
    greeted = False
    steps = list(range(n - 1, 0, -1))
    for slot in range(held):
        for step in steps:
            target = partner(me, step, n)[0]
            cross, packed, last = gram(target * held + slot)
            place = out_buf.at[step - 1, slot]
            place[:half, :] = cross.astype(BF16)
            place[half : 2 * half, :] = packed.astype(BF16)
            place[2 * half :, :] = jnp.broadcast_to(last, (16, half)).astype(BF16)
            if not greeted:
                pl.semaphore_wait(barrier, n - 1)
                greeted = True
            copy = pltpu.make_async_remote_copy(
                src_ref=place,
                dst_ref=in_buf.at[step - 1, slot],
                send_sem=rs_send.at[step - 1, slot],
                recv_sem=rs_recv.at[step - 1, slot],
                device_id={"rep": target},
                device_id_type=MESH,
            )
            copy.start()
            rs[step, slot] = copy
        cross, packed, last = gram(me * held + slot)
        own_f[slot, :half, :] = cross
        own_f[slot, half : 2 * half, :] = packed
        own_f[slot, 2 * half :, :] = jnp.broadcast_to(last, (8, half))

    loads[1].wait()
    widen(grads_v, grads_f)
    loads[2].wait()

    eye = jnp.where(
        lax.broadcasted_iota(jnp.int32, (order, order), 0)
        == lax.broadcasted_iota(jnp.int32, (order, order), 1),
        1.0,
        0.0,
    ).astype(F32)

    ag = {}

    def ship(key, source, target, step, sem):
        copy = pltpu.make_async_remote_copy(
            src_ref=source,
            dst_ref=target,
            send_sem=ag_send.at[sem],
            recv_sem=ag_recv.at[sem],
            device_id={"rep": partner(me, step, n)[0]},
            device_id_type=MESH,
        )
        copy.start()
        ag[key] = copy

    def refresh_block(slot):
        total = own_f[slot]
        total_cross, total_packed, total_last = (
            total[:half],
            total[half : 2 * half],
            total[2 * half : 2 * half + 1],
        )
        for step in steps:
            rs[step, slot].wait_recv()
            came = in_buf[step - 1, slot].astype(F32)
            total_cross = total_cross + came[:half]
            total_packed = total_packed + came[half : 2 * half]
            total_last = total_last + came[2 * half : 2 * half + 1]
        scale = 1.0 / tokens_all
        flipped = total_packed.T
        first = jnp.where(upper, total_packed, flipped)
        second = jnp.where(
            on_diag,
            jnp.broadcast_to(total_last, (half, half)),
            jnp.where(upper, flipped, total_packed),
        )
        covariance = (
            jnp.concatenate(
                [
                    jnp.concatenate([first, total_cross], axis=1),
                    jnp.concatenate([total_cross.T, second], axis=1),
                ],
                axis=0,
            )
            * scale
        )
        cov_ref[slot] = covariance
        matrix = covariance + damping_ref[slot] * eye
        bound = jnp.max(jnp.sum(jnp.abs(matrix), axis=0, keepdims=True), axis=1, keepdims=True)
        inverse_bound = 1.0 / bound
        residual = eye - matrix * inverse_bound
        series = eye + residual
        power = split(residual)
        power = split(dot3(power, power))
        for iteration in range(2, ITERS):
            left = split(series)
            square = dot3(power, power)
            series = series + dot3(left, power)
            power = split(square)
        series = series + dot3(split(series), power)
        approx = (series * inverse_bound).astype(BF16)
        due = jnp.full((order, order), refresh_ref[slot], jnp.int32) != groups
        chosen = jnp.where(due, approx, old_v[slot])
        inv_ref[slot] = chosen
        gathered[0, slot] = chosen
        if relay:
            top, bottom = pl.ds(0, halves), pl.ds(halves, halves)
            for part, (step, piece) in enumerate(((1, top), (2, bottom), (1, bottom), (2, top))):
                ship(
                    (slot, part),
                    gathered.at[0, slot, piece],
                    gathered.at[step, slot, piece],
                    step,
                    slot * 6 + part,
                )
        else:
            for step in steps:
                ship(
                    (slot, step),
                    gathered.at[0, slot],
                    gathered.at[step, slot],
                    step,
                    slot * 6 * n + step,
                )

    def forward(slot):
        top, bottom = pl.ds(0, halves), pl.ds(halves, halves)
        ag[slot, 0].wait_recv()
        ship((slot, 4), gathered.at[1, slot, top], gathered.at[3, slot, top], 2, slot * 6 + 4)
        ag[slot, 1].wait_recv()
        ship((slot, 5), gathered.at[2, slot, bottom], gathered.at[3, slot, bottom], 1, slot * 6 + 5)

    def apply(step, slot):
        block = partner(me, step, n)[1] * held + slot
        result = jnp.dot(
            take(grads_f, block), gathered[step, slot], preferred_element_type=F32
        )
        for tile in range(order // 128):
            pre_f[tile, pl.ds(block, rows, stride=blocks), :] = result[
                :, tile * 128 : (tile + 1) * 128
            ]

    for slot in range(held):
        refresh_block(slot)
        if relay and slot > 0:
            forward(slot - 1)
    if relay:
        forward(held - 1)
    for slot in range(held):
        apply(0, slot)
    for slot in range(held):
        if relay:
            ag[slot, 2].wait_recv()
            apply(1, slot)
            ag[slot, 3].wait_recv()
            apply(2, slot)
            ag[slot, 4].wait_recv()
            ag[slot, 5].wait_recv()
            apply(3, slot)
        else:
            for step in steps:
                ag[slot, step].wait_recv()
                apply(step, slot)
    for copy in rs.values():
        copy.wait_send()
    for copy in ag.values():
        copy.wait_send()


def deliver(cov_v, inv_v, wide, cov_hbm, inv_hbm, pre_hbm, narrow, sem):
    copies = [
        pltpu.make_async_copy(cov_v, cov_hbm, sem.at[0]),
        pltpu.make_async_copy(inv_v, inv_hbm, sem.at[1]),
    ]
    for copy in copies:
        copy.start()
    size = narrow.shape[0] // CHUNKS
    for chunk in range(CHUNKS):
        part = pl.ds(chunk * size, size)
        for tile in range(wide.shape[0]):
            narrow[part, tile * 128 : (tile + 1) * 128] = wide[tile, part, :].astype(BF16)
        copy = pltpu.make_async_copy(narrow.at[part], pre_hbm.at[part], sem.at[2 + chunk])
        copy.start()
        copies.append(copy)
    for copy in copies:
        copy.wait()


def local(acts, refresh, damping, old_inverse, grads):
    n = lax.axis_size("rep")
    groups = lax.axis_size("mp")
    rows, blocks, order = acts.shape
    grad_rows = grads.shape[0]
    held = refresh.shape[0]
    half = order // 2
    tiles = order // 128
    copies = held * 6 if n == 4 else held * 6 * n
    any_space = pl.BlockSpec(memory_space=pltpu.HBM)
    smem = pl.BlockSpec(memory_space=pltpu.SMEM)
    vmem = pl.BlockSpec(memory_space=pltpu.VMEM)
    scratch = [
        pltpu.VMEM((rows * blocks, order), BF16),
        pltpu.VMEM((grad_rows * blocks, order), BF16),
        pltpu.VMEM((held, order, order), BF16),
        pltpu.VMEM((tiles, rows * blocks, 128), F32),
        pltpu.VMEM((tiles, grad_rows * blocks, 128), F32),
        pltpu.VMEM((held, order + 8, half), F32),
        pltpu.VMEM((n - 1, held, order + 16, half), BF16),
        pltpu.VMEM((n - 1, held, order + 16, half), BF16),
        pltpu.VMEM((n, held, order, order), BF16),
        pltpu.SemaphoreType.DMA((3,)),
        pltpu.SemaphoreType.DMA((n - 1, held)),
        pltpu.SemaphoreType.DMA((n - 1, held)),
        pltpu.SemaphoreType.DMA((copies,)),
        pltpu.SemaphoreType.DMA((copies,)),
        ]
    need = sum(
        math.prod(item.shape) * jnp.dtype(item.dtype).itemsize
        for item in scratch
        if item.memory_space == pltpu.VMEM
    )
    covariance, new_inverse, wide = pl.pallas_call(
        functools.partial(kernel, n, held, groups, rows * n),
        out_shape=(
            pltpu.VMEM((held, order, order), F32),
            pltpu.VMEM((held, order, order), BF16),
            pltpu.VMEM((tiles, grad_rows * blocks, 128), F32),
        ),
        in_specs=[any_space, smem, smem, any_space, any_space],
        out_specs=(vmem, vmem, vmem),
        scratch_shapes=scratch,
        compiler_params=pltpu.CompilerParams(
            collective_id=0, has_side_effects=True, vmem_limit_bytes=need + (8 << 20)
        ),
    )(
        pltpu.with_memory_space_constraint(acts.reshape(rows * blocks, order), pltpu.HBM),
        pltpu.with_memory_space_constraint(refresh, pltpu.HBM),
        pltpu.with_memory_space_constraint(damping, pltpu.HBM),
        pltpu.with_memory_space_constraint(old_inverse, pltpu.HBM),
        pltpu.with_memory_space_constraint(grads.reshape(grad_rows * blocks, order), pltpu.HBM),
    )
    covariance, new_inverse, precond = pl.pallas_call(
        deliver,
        out_shape=(
            jax.ShapeDtypeStruct((held, order, order), F32),
            jax.ShapeDtypeStruct((held, order, order), BF16),
            jax.ShapeDtypeStruct((grad_rows * blocks, order), BF16),
        ),
        in_specs=[vmem] * 3,
        out_specs=(any_space,) * 3,
        scratch_shapes=[
            pltpu.VMEM((grad_rows * blocks, order), BF16),
            pltpu.SemaphoreType.DMA((2 + CHUNKS,)),
        ],
        compiler_params=pltpu.CompilerParams(
            vmem_limit_bytes=grad_rows * blocks * order * 2 + (2 << 20)
        ),
    )(covariance, new_inverse, wide)
    return covariance, new_inverse, precond.reshape(grad_rows, blocks, order)


def solution(mesh):
    return jax.shard_map(
        local,
        mesh=mesh,
        in_specs=(
            P("rep", "mp", None),
            P(("mp", "rep")),
            P(("mp", "rep")),
            P(("mp", "rep"), None, None),
            P("rep", "mp", None),
        ),
        out_specs=(
            P(("mp", "rep"), None, None),
            P(("mp", "rep"), None, None),
            P("rep", "mp", None),
        ),
        check_vma=False,
    )
```

```python
import functools
import math

import jax
import jax.numpy as jnp
from jax import lax
from jax.experimental import pallas as pl
from jax.experimental.pallas import tpu as pltpu
from jax.sharding import PartitionSpec as P

ITERS = 5
CHUNKS = 4
LOADS = 4
MESH = pl.DeviceIdType.MESH
F32 = jnp.float32
BF16 = jnp.bfloat16


def split(x):
    high = x.astype(BF16)
    return high, (x - high.astype(F32)).astype(BF16)


def dot3(lhs, rhs):
    lh, ll = lhs
    rh, rl = rhs
    mm = functools.partial(jnp.dot, preferred_element_type=F32)
    return mm(lh, rh) + (mm(lh, rl) + mm(ll, rh))


def partner(me, step, n):
    if n & (n - 1):
        return lax.rem(me + step, n), lax.rem(me + n - step, n)
    other = me
    bit = 1
    while bit < n:
        if step & bit:
            other = other + bit * (1 - 2 * lax.rem(me // bit, 2))
        bit *= 2
    return other, other


def kernel(
    n,
    held,
    groups,
    tokens_all,
    acts_hbm,
    refresh_ref,
    damping_ref,
    old_hbm,
    grads_hbm,
    cov_ref,
    inv_ref,
    pre_f,
    acts_v,
    grads_v,
    old_v,
    acts_f,
    grads_f,
    own_f,
    out_buf,
    in_buf,
    gathered,
    load_sem,
    rs_send,
    rs_recv,
    ag_send,
    ag_recv,
):
    me = lax.axis_index("rep")
    blocks = n * held
    order = inv_ref.shape[-1]
    half = order // 2
    rows = acts_v.shape[0] // blocks
    relay = n == 4
    halves = order // 2

    barrier = pltpu.get_barrier_semaphore()
    for step in range(1, n):
        pl.semaphore_signal(
            barrier, inc=1, device_id={"rep": partner(me, step, n)[0]}, device_id_type=MESH
        )

    piece = acts_v.shape[0] // LOADS
    loads = [
        pltpu.make_async_copy(acts_hbm.at[pl.ds(c * piece, piece)], acts_v.at[pl.ds(c * piece, piece)], load_sem.at[3 + c])
        for c in range(LOADS)
    ] + [
        pltpu.make_async_copy(grads_hbm, grads_v, load_sem.at[1]),
        pltpu.make_async_copy(old_hbm, old_v, load_sem.at[2]),
    ]
    for load in loads:
        load.start()

    row_id = lax.broadcasted_iota(jnp.int32, (half, half), 0)
    col_id = lax.broadcasted_iota(jnp.int32, (half, half), 1)
    upper = col_id >= row_id
    on_diag = col_id == row_id

    def widen(source, target):
        for tile in range(order // 128):
            target[tile] = source[:, tile * 128 : (tile + 1) * 128].astype(F32)

    def take(source, block):
        return jnp.concatenate(
            [
                source[tile, pl.ds(block, rows, stride=blocks), :]
                for tile in range(order // 128)
            ],
            axis=1,
        ).astype(BF16)

    def gram(block):
        part = take(acts_f, block)
        full = lax.dot_general(
            part, part, (((0,), (0,)), ((), ())), preferred_element_type=F32
        )
        low = full[half:, half:]
        last = jnp.sum(jnp.where(on_diag, low, 0.0), axis=0, keepdims=True)
        return full[:half, half:], jnp.where(upper, full[:half, :half], low), last

    for c in range(LOADS):
        loads[c].wait()
        part = pl.ds(c * piece, piece)
        for tile in range(order // 128):
            acts_f[tile, part, :] = acts_v[part, tile * 128 : (tile + 1) * 128].astype(F32)

    rs = {}
    greeted = False
    steps = list(range(n - 1, 0, -1))
    for slot in range(held):
        for step in steps:
            target = partner(me, step, n)[0]
            cross, packed, last = gram(target * held + slot)
            place = out_buf.at[step - 1, slot]
            place[:half, :] = cross.astype(BF16)
            place[half : 2 * half, :] = packed.astype(BF16)
            place[2 * half :, :] = jnp.broadcast_to(last, (16, half)).astype(BF16)
            if not greeted:
                pl.semaphore_wait(barrier, n - 1)
                greeted = True
            copy = pltpu.make_async_remote_copy(
                src_ref=place,
                dst_ref=in_buf.at[step - 1, slot],
                send_sem=rs_send.at[step - 1, slot],
                recv_sem=rs_recv.at[step - 1, slot],
                device_id={"rep": target},
                device_id_type=MESH,
            )
            copy.start()
            rs[step, slot] = copy
        cross, packed, last = gram(me * held + slot)
        own_f[slot, :half, :] = cross
        own_f[slot, half : 2 * half, :] = packed
        own_f[slot, 2 * half :, :] = jnp.broadcast_to(last, (8, half))

    loads[LOADS].wait()
    widen(grads_v, grads_f)
    loads[LOADS + 1].wait()

    eye = jnp.where(
        lax.broadcasted_iota(jnp.int32, (order, order), 0)
        == lax.broadcasted_iota(jnp.int32, (order, order), 1),
        1.0,
        0.0,
    ).astype(F32)

    ag = {}
    settled = set()

    def ship(key, source, target, step, sem):
        copy = pltpu.make_async_remote_copy(
            src_ref=source,
            dst_ref=target,
            send_sem=ag_send.at[sem],
            recv_sem=ag_recv.at[sem],
            device_id={"rep": partner(me, step, n)[0]},
            device_id_type=MESH,
        )
        copy.start()
        ag[key] = copy

    def refresh_block(slot):
        total = own_f[slot]
        total_cross, total_packed, total_last = (
            total[:half],
            total[half : 2 * half],
            total[2 * half : 2 * half + 1],
        )
        for step in steps:
            rs[step, slot].wait_recv()
            came = in_buf[step - 1, slot].astype(F32)
            total_cross = total_cross + came[:half]
            total_packed = total_packed + came[half : 2 * half]
            total_last = total_last + came[2 * half : 2 * half + 1]
        scale = 1.0 / tokens_all
        flipped = total_packed.T
        first = jnp.where(upper, total_packed, flipped)
        second = jnp.where(
            on_diag,
            jnp.broadcast_to(total_last, (half, half)),
            jnp.where(upper, flipped, total_packed),
        )
        covariance = (
            jnp.concatenate(
                [
                    jnp.concatenate([first, total_cross], axis=1),
                    jnp.concatenate([total_cross.T, second], axis=1),
                ],
                axis=0,
            )
            * scale
        )
        cov_ref[slot] = covariance
        matrix = covariance + damping_ref[slot] * eye
        bound = jnp.max(jnp.sum(jnp.abs(matrix), axis=0, keepdims=True), axis=1, keepdims=True)
        inverse_bound = 1.0 / bound
        residual = eye - matrix * inverse_bound
        series = eye + residual
        power = split(residual)
        power = split(dot3(power, power))
        for iteration in range(2, ITERS):
            left = split(series)
            square = dot3(power, power)
            series = series + dot3(left, power)
            power = split(square)
        series = series + dot3(split(series), power)
        approx = (series * inverse_bound).astype(BF16)
        due = jnp.full((order, order), refresh_ref[slot], jnp.int32) != groups
        chosen = jnp.where(due, approx, old_v[slot])
        inv_ref[slot] = chosen
        gathered[0, slot] = chosen
        if relay:
            top, bottom = pl.ds(0, halves), pl.ds(halves, halves)
            for part, (step, piece) in enumerate(((1, top), (2, bottom), (1, bottom), (2, top))):
                if part == 2 and slot > 0:
                    for sent in (0, 1):
                        ag[slot, sent].wait_send()
                        settled.add((slot, sent))
                    forward(slot - 1)
                ship(
                    (slot, part),
                    gathered.at[0, slot, piece],
                    gathered.at[step, slot, piece],
                    step,
                    slot * 6 + part,
                )
        else:
            for step in steps:
                ship(
                    (slot, step),
                    gathered.at[0, slot],
                    gathered.at[step, slot],
                    step,
                    slot * 6 * n + step,
                )

    def forward(slot):
        top, bottom = pl.ds(0, halves), pl.ds(halves, halves)
        ag[slot, 0].wait_recv()
        ship((slot, 4), gathered.at[1, slot, top], gathered.at[3, slot, top], 2, slot * 6 + 4)
        ag[slot, 1].wait_recv()
        ship((slot, 5), gathered.at[2, slot, bottom], gathered.at[3, slot, bottom], 1, slot * 6 + 5)

    def apply(step, slot):
        block = partner(me, step, n)[1] * held + slot
        result = jnp.dot(
            take(grads_f, block), gathered[step, slot], preferred_element_type=F32
        )
        for tile in range(order // 128):
            pre_f[tile, pl.ds(block, rows, stride=blocks), :] = result[
                :, tile * 128 : (tile + 1) * 128
            ]

    for slot in range(held):
        refresh_block(slot)
    if relay:
        forward(held - 1)
    for slot in range(held):
        apply(0, slot)
    for slot in range(held):
        if relay:
            ag[slot, 2].wait_recv()
            apply(1, slot)
            ag[slot, 3].wait_recv()
            apply(2, slot)
            ag[slot, 4].wait_recv()
            ag[slot, 5].wait_recv()
            apply(3, slot)
        else:
            for step in steps:
                ag[slot, step].wait_recv()
                apply(step, slot)
    for copy in rs.values():
        copy.wait_send()
    for key, copy in ag.items():
        if key not in settled:
            copy.wait_send()


def deliver(cov_v, inv_v, wide, cov_hbm, inv_hbm, pre_hbm, narrow, sem):
    copies = [
        pltpu.make_async_copy(cov_v, cov_hbm, sem.at[0]),
        pltpu.make_async_copy(inv_v, inv_hbm, sem.at[1]),
    ]
    for copy in copies:
        copy.start()
    size = narrow.shape[0] // CHUNKS
    for chunk in range(CHUNKS):
        part = pl.ds(chunk * size, size)
        for tile in range(wide.shape[0]):
            narrow[part, tile * 128 : (tile + 1) * 128] = wide[tile, part, :].astype(BF16)
        copy = pltpu.make_async_copy(narrow.at[part], pre_hbm.at[part], sem.at[2 + chunk])
        copy.start()
        copies.append(copy)
    for copy in copies:
        copy.wait()


def local(acts, refresh, damping, old_inverse, grads):
    n = lax.axis_size("rep")
    groups = lax.axis_size("mp")
    rows, blocks, order = acts.shape
    grad_rows = grads.shape[0]
    held = refresh.shape[0]
    half = order // 2
    tiles = order // 128
    copies = held * 6 if n == 4 else held * 6 * n
    any_space = pl.BlockSpec(memory_space=pltpu.HBM)
    smem = pl.BlockSpec(memory_space=pltpu.SMEM)
    vmem = pl.BlockSpec(memory_space=pltpu.VMEM)
    scratch = [
        pltpu.VMEM((rows * blocks, order), BF16),
        pltpu.VMEM((grad_rows * blocks, order), BF16),
        pltpu.VMEM((held, order, order), BF16),
        pltpu.VMEM((tiles, rows * blocks, 128), F32),
        pltpu.VMEM((tiles, grad_rows * blocks, 128), F32),
        pltpu.VMEM((held, order + 8, half), F32),
        pltpu.VMEM((n - 1, held, order + 16, half), BF16),
        pltpu.VMEM((n - 1, held, order + 16, half), BF16),
        pltpu.VMEM((n, held, order, order), BF16),
        pltpu.SemaphoreType.DMA((3 + LOADS,)),
        pltpu.SemaphoreType.DMA((n - 1, held)),
        pltpu.SemaphoreType.DMA((n - 1, held)),
        pltpu.SemaphoreType.DMA((copies,)),
        pltpu.SemaphoreType.DMA((copies,)),
        ]
    need = sum(
        math.prod(item.shape) * jnp.dtype(item.dtype).itemsize
        for item in scratch
        if item.memory_space == pltpu.VMEM
    )
    covariance, new_inverse, wide = pl.pallas_call(
        functools.partial(kernel, n, held, groups, rows * n),
        out_shape=(
            pltpu.VMEM((held, order, order), F32),
            pltpu.VMEM((held, order, order), BF16),
            pltpu.VMEM((tiles, grad_rows * blocks, 128), F32),
        ),
        in_specs=[any_space, smem, smem, any_space, any_space],
        out_specs=(vmem, vmem, vmem),
        scratch_shapes=scratch,
        compiler_params=pltpu.CompilerParams(
            collective_id=0, has_side_effects=True, vmem_limit_bytes=need + (8 << 20)
        ),
    )(
        pltpu.with_memory_space_constraint(acts.reshape(rows * blocks, order), pltpu.HBM),
        pltpu.with_memory_space_constraint(refresh, pltpu.HBM),
        pltpu.with_memory_space_constraint(damping, pltpu.HBM),
        pltpu.with_memory_space_constraint(old_inverse, pltpu.HBM),
        pltpu.with_memory_space_constraint(grads.reshape(grad_rows * blocks, order), pltpu.HBM),
    )
    covariance, new_inverse, precond = pl.pallas_call(
        deliver,
        out_shape=(
            jax.ShapeDtypeStruct((held, order, order), F32),
            jax.ShapeDtypeStruct((held, order, order), BF16),
            jax.ShapeDtypeStruct((grad_rows * blocks, order), BF16),
        ),
        in_specs=[vmem] * 3,
        out_specs=(any_space,) * 3,
        scratch_shapes=[
            pltpu.VMEM((grad_rows * blocks, order), BF16),
            pltpu.SemaphoreType.DMA((2 + CHUNKS,)),
        ],
        compiler_params=pltpu.CompilerParams(
            vmem_limit_bytes=grad_rows * blocks * order * 2 + (2 << 20)
        ),
    )(covariance, new_inverse, wide)
    return covariance, new_inverse, precond.reshape(grad_rows, blocks, order)


def solution(mesh):
    return jax.shard_map(
        local,
        mesh=mesh,
        in_specs=(
            P("rep", "mp", None),
            P(("mp", "rep")),
            P(("mp", "rep")),
            P(("mp", "rep"), None, None),
            P("rep", "mp", None),
        ),
        out_specs=(
            P(("mp", "rep"), None, None),
            P(("mp", "rep"), None, None),
            P("rep", "mp", None),
        ),
        check_vma=False,
    )
```
